32 devices in a mesh: groups: 2 (over x), space: 16 (over z, y, core).
Axes of the slice: x: 2, y: 2, z: 4, core: 2. Of those that a mesh axis runs over, the one named last changes fastest.
Arguments:
- volume: bfloat16 [64, 64, 32, 64], P(('groups', 'space')), parts along dimension 0, may hold values from -6 to 6
- weight_one: bfloat16 [3, 3, 3, 64, 64], replicated, may hold values from -0.15625 to 0.15625
- weight_two: bfloat16 [3, 3, 3, 64, 128], replicated, may hold values from -0.15625 to 0.15625
- cotangent: bfloat16 [64, 64, 32, 128], P(('groups', 'space')), parts along dimension 0, may hold values from -6 to 6
Outputs:
- output: float32 [64, 64, 32, 128], P(('groups', 'space')), parts along dimension 0
- grad_volume: float32 [64, 64, 32, 64], P(('groups', 'space')), parts along dimension 0
- grad_one: float32 [6, 3, 3, 64, 64], P('groups', None, None, None, 'space'), parts along dimension 0
- grad_two: float32 [6, 3, 3, 64, 128], P('groups', None, None, None, 'space'), parts along dimension 0
The draws below stay inside these ranges and needn't reach their ends.
There are 2 independent parts, one for each index of `groups`. The reference program is written for one: setup_inputs(seed, part) draws one part's arguments, and reference() takes and returns one part's arrays. A program takes and returns all parts, laid end to end along the dimension named above; an argument that names none is the same for every part. Nothing has to cross between parts.
All inputs are finite; a program needn't handle non-finite values.
Results may differ from the reference program's by a relative error of at most 0.0029.
Values may be sent and summed in bfloat16 or wider, within the bound.
A program may use at most 64 MiB of HBM per device.

```python
import math
import jax
import jax.numpy as jnp
from jax import lax

CH_IN = 64
CH_MID = 64
CH_OUT = 128
HEIGHT = 64
WIDTH = 32
DEPTH = 32
CELLS = 65536


def raised(result, own_key, source, target, parts, factor):
    owner, partner = [(jnp.arange(result.shape[dim]) // (result.shape[dim] // parts)).reshape([-1 if axis == dim else 1 for axis in range(result.ndim)]) for dim in (source, target)]
    chosen = jax.random.permutation(own_key, parts)[partner]
    strong = (owner == chosen) | (owner == (partner + parts // 2) % parts)
    return jnp.where(strong, factor * result, result)


def block_levels(key, extent, cuts, smallest, top_value):
    def one(axis_at, blocks):
        heights = jax.random.uniform(jax.random.fold_in(jax.random.fold_in(key, 6), axis_at), (blocks,), jnp.float32, smallest / len(cuts), top_value / len(cuts))
        return jnp.repeat(jnp.exp(heights), extent[axis_at] // blocks).reshape((-1,) + (1,) * (len(extent) - axis_at - 1))

    loudness = one(*cuts[0])
    for cut in cuts[1:]:
        loudness = loudness * one(*cut)
    return loudness


def scatter_about(key, extent, spread, limit, cuts=(), kind=jnp.bfloat16):
    array = spread * jax.random.normal(key, extent, jnp.float32)
    if cuts:
        array = array * block_levels(key, extent, cuts, -0.22, 0.18)
    return jnp.clip(array, -limit, limit).astype(kind)


def gaussian_with(rng, shape, scale, reach, cuts, heavy, kind=jnp.bfloat16):
    values = scale * jax.random.normal(rng, shape, jnp.float32)
    if cuts:
        values = values * block_levels(rng, shape, cuts, -0.22, 0.18)
    return jnp.clip(raised(values, jax.random.fold_in(rng, 3), *heavy), -reach, reach).astype(kind)


def setup_inputs(seed: int = 0, part: int = 0) -> dict:
    key_of = jax.random.split(jax.random.key(seed), 5)
    part_keys = jax.random.split(jax.random.fold_in(key_of[4], part), 5)
    volume = scatter_about(part_keys[0], (DEPTH, HEIGHT, WIDTH, CH_IN), 1.0, 6.0, ((0, 16),))
    weight_one = scatter_about(key_of[1], (3, 3, 3, CH_IN, CH_MID), (27 * CH_IN) ** -0.5, 0.15625)
    weight_two = scatter_about(key_of[2], (3, 3, 3, CH_MID, CH_OUT), (27 * CH_MID) ** -0.5, 0.15625)
    cotangent = gaussian_with(part_keys[3], (DEPTH, HEIGHT, WIDTH, CH_OUT), 1.0, 6.0, ((0, 16),), (0, 3, 16, 2.0))
    return dict(volume=volume, weight_one=weight_one, weight_two=weight_two, cotangent=cotangent)


def pad_cells(field):
    return jnp.pad(field, ((1, 1), (1, 1), (1, 1), (0, 0)))

def conv_valid(padded, kernel):
    return lax.conv_general_dilated(padded[None], kernel, (1, 1, 1), 'VALID', dimension_numbers=('NDHWC', 'DHWIO', 'NDHWC'), precision=lax.Precision.HIGHEST)[0]

def flipped(kernel):
    return jnp.transpose(kernel[::-1, ::-1, ::-1], (0, 1, 2, 4, 3))

def kernel_terms(padded, grad_field):
    depth_len, rows_len, cols_len = (grad_field.shape[0], grad_field.shape[1], grad_field.shape[2])
    flat_grad = grad_field.reshape(-1, grad_field.shape[3])
    results = []
    for depth_tap in range(3):
        for row_tap in range(3):
            for column_tap in range(3):
                window = padded[depth_tap:depth_tap + depth_len, row_tap:row_tap + rows_len, column_tap:column_tap + cols_len]
                results.append(lax.dot_general(window.reshape(-1, padded.shape[3]), flat_grad, (((0,), (0,)), ((), ())), precision=lax.Precision.HIGHEST))
    return jnp.stack(results).reshape(3, 3, 3, padded.shape[3], grad_field.shape[3])

def reference(volume, weight_one, weight_two, cotangent):
    inputs = volume.astype(jnp.float32)
    kernel_one = weight_one.astype(jnp.float32)
    kernel_two = weight_two.astype(jnp.float32)
    grad_out = cotangent.astype(jnp.float32)
    hidden = conv_valid(pad_cells(inputs), kernel_one)
    sigmoid_hidden = jax.nn.sigmoid(hidden)
    activation = (hidden * sigmoid_hidden).astype(jnp.bfloat16).astype(jnp.float32)
    output = conv_valid(pad_cells(activation), kernel_two)
    grad_act = conv_valid(pad_cells(grad_out), flipped(kernel_two))
    grad_hidden = (grad_act * sigmoid_hidden * (1.0 + hidden * (1.0 - sigmoid_hidden))).astype(jnp.bfloat16).astype(jnp.float32)
    grad_volume = conv_valid(pad_cells(grad_hidden), flipped(kernel_one))
    scale = 1.0 / math.sqrt(CELLS)
    grad_one = kernel_terms(pad_cells(inputs), grad_hidden) * scale
    grad_two = kernel_terms(pad_cells(activation), grad_out) * scale
    return (output, grad_volume, grad_one, grad_two)
```

```python
import functools
import math

import jax
import jax.numpy as jnp
from jax import lax
from jax.experimental import pallas as pl
from jax.experimental.pallas import tpu as pltpu
from jax.sharding import PartitionSpec as P

MESH = pl.DeviceIdType.MESH
F32 = jnp.float32
BF16 = jnp.bfloat16
TN = (((0,), (0,)), ((), ()))


def kernel(
    n, planes, height, width, ci, cm, co, scale,
    vol, cot, w1_in, w2_in,
    out_hbm, gvol_hbm, g1, g2,
    out, gvol, pv, pa, pg, ct, vraw, cs, cr, hid, dsl, back, ctt, ght, acc1, acc2,
    w1, w2, k1, k1f, k2, wg, own, tx, rx, ty, ry,
    loc_sem, st_sem, hs_sem, hr_sem, ps_sem, pr_sem, ts_sem, tr_sem,
):
    me = lax.axis_index("space")
    plane = height * width
    chunk = plane // 4
    pad = plane + 2 * width
    half = height // 2
    step_rows = chunk // (2 * width)
    r1, r2 = cm // n, co // n

    barrier = pltpu.get_barrier_semaphore()
    for j in range(1, n):
        pl.semaphore_signal(
            barrier, inc=1, device_id={"space": lax.rem(me + j, n)}, device_id_type=MESH
        )

    local = [pltpu.make_async_copy(vol, vraw, loc_sem.at[0])]
    for p in range(planes):
        local.append(
            pltpu.make_async_copy(
                cot.at[pl.ds(p * plane, plane)],
                ct.at[p, pl.ds(width, plane)],
                loc_sem.at[1 + p],
            )
        )
    weights = [
        pltpu.make_async_copy(w2_in, w2, loc_sem.at[1 + planes]),
        pltpu.make_async_copy(w1_in, w1, loc_sem.at[2 + planes]),
    ]
    for copy in local[:1] + weights + local[1:]:
        copy.start()

    for ref in (pv, pa, pg):
        zero = jnp.zeros((width, ref.shape[4]), BF16)
        for p in range(planes + 2):
            ref[p, 0, 0] = zero
            ref[p, half, 0] = zero
            ref[p, half, 1] = zero
    zero = jnp.zeros((width, co), BF16)
    for p in range(planes):
        ct[p, pl.ds(0, width), :] = zero
        ct[p, pl.ds(pad - width, width), :] = zero

    def place(ref, p, k, x, c):
        m = k * step_rows
        x = x.reshape(step_rows, 2, width, c)
        ref[p, pl.ds(m, step_rows), :, :, c:] = x
        ref[p, pl.ds(m, step_rows), 1, :, :c] = x[:, 0]
        ref[p, pl.ds(m + 1, step_rows), 0, :, :c] = x[:, 1]

    def chunks(body, count=4):
        def step(k, carry):
            body(k, pl.multiple_of(k * chunk, chunk))
            return carry

        lax.fori_loop(0, count, step, 0)

    def fill(ref, p, c):
        x = ref[p, pl.ds(0, half), 1]
        ref[p, pl.ds(1, half), 0, :, :c] = x[:, :, c:]
        ref[p, pl.ds(0, half), 0, :, c:] = x[:, :, :c]

    local[0].wait()
    for p in range(planes):

        def own_volume(k, row, p=p):
            at = pl.ds(pl.multiple_of(p * plane + row, chunk), chunk)
            place(pv, p + 1, k, vraw[at, :], ci)

        chunks(own_volume)

    def halo(kind, low_src, high_src, low_dst, high_dst):
        left = pltpu.make_async_remote_copy(
            low_src, high_dst, hs_sem.at[kind, 0], hr_sem.at[kind, 0],
            device_id={"space": lax.rem(me + n - 1, n)}, device_id_type=MESH,
        )
        right = pltpu.make_async_remote_copy(
            high_src, low_dst, hs_sem.at[kind, 1], hr_sem.at[kind, 1],
            device_id={"space": lax.rem(me + 1, n)}, device_id_type=MESH,
        )

        def start():
            @pl.when(me > 0)
            def _():
                left.start()

            @pl.when(me < n - 1)
            def _():
                right.start()

        def wait_recv():
            @pl.when(me < n - 1)
            def _():
                left.wait_recv()

            @pl.when(me == n - 1)
            def _():
                high_dst[...] = jnp.zeros(high_dst.shape, BF16)

            @pl.when(me > 0)
            def _():
                right.wait_recv()

            @pl.when(me == 0)
            def _():
                low_dst[...] = jnp.zeros(low_dst.shape, BF16)

        def wait_send():
            @pl.when(me > 0)
            def _():
                left.wait_send()

            @pl.when(me < n - 1)
            def _():
                right.wait_send()

        return start, wait_recv, wait_send

    def field_halo(kind, ref):
        whole = pl.ds(0, half)
        return halo(
            kind,
            ref.at[1, whole, 1], ref.at[planes, whole, 1],
            ref.at[0, whole, 1], ref.at[planes + 1, whole, 1],
        )

    volume_halo = field_halo(0, pv)
    cot_halo = halo(1, cs.at[0], cs.at[1], cr.at[0], cr.at[1])
    act_halo = field_halo(2, pa)
    grad_halo = field_halo(3, pg)

    pl.semaphore_wait(barrier, n - 1)
    volume_halo[0]()

    for copy in weights:
        copy.wait()

    for t in range(9):
        w = w2[8 - t]
        order = [w[2 * cm :], w[:cm], w[cm : 2 * cm]]
        wg[pl.ds(t * co, co), :] = jnp.concatenate(order, axis=0).T
        a, b = t // 3, t % 3
        w = w1[8 - t]
        order = [w[2 * ci :], w[:ci], w[ci : 2 * ci]]
        k1f[a, pl.ds(b * cm, cm), :] = jnp.concatenate(order, axis=0).T
        w = w1[t]
        order = [w[:ci], w[2 * ci :], w[ci : 2 * ci]]
        k1[a, pl.ds(b * ci, ci), :] = jnp.concatenate(order, axis=1)
        w = w2[t]
        order = [w[:cm], w[cm : 2 * cm], w[2 * cm :]]
        k2[a, pl.ds(b * cm, cm), :] = jnp.concatenate(order, axis=1)
    for a in range(3):
        k1[a, pl.ds(3 * ci, ci), :] = jnp.zeros((ci, 3 * cm), BF16)
        k1f[a, pl.ds(3 * cm, cm), :] = jnp.zeros((cm, 3 * ci), BF16)
        k2[a, pl.ds(3 * cm, cm), :] = jnp.zeros((cm, 3 * co), BF16)

    column = lax.broadcasted_iota(jnp.int32, (chunk, 1), 0) % width
    first = column == 0
    last = column == width - 1
    low_lanes = lax.broadcasted_iota(jnp.int32, (1, 2 * cm), 1) < cm

    def from_left(x):
        return jnp.where(first, 0.0, pltpu.roll(x, 1, 0))

    def from_right(x):
        return jnp.where(last, 0.0, pltpu.roll(x, chunk - 1, 0))

    def narrow(y):
        c = y.shape[1] // 3
        z = y[:, : 2 * c]
        z = jnp.where(low_lanes, from_left(z), from_right(z))
        return z[:, :c] + z[:, c:] + y[:, 2 * c :]

    def wide(y):
        c = y.shape[1] // 3
        return from_left(y[:, :c]) + y[:, c : 2 * c] + from_right(y[:, 2 * c :])

    def window(ref, p, k):
        m = k * step_rows
        low = ref[p, pl.ds(m, step_rows)].reshape(chunk, ref.shape[4])
        high = ref[p, pl.ds(m + 1, step_rows)].reshape(chunk, ref.shape[4])
        return jnp.concatenate([low, high], axis=1)

    def conv(ref, kernels, p, k, taps):
        total = None
        for a in taps:
            term = jnp.dot(window(ref, p + a, k), kernels[a], preferred_element_type=F32)
            total = term if total is None else total + term
        return total

    def back_terms(p, row, low_tap, source, count):
        pieces = [
            ct[q, pl.ds(pl.multiple_of(row + b * width, width), chunk), :]
            for q in range(source, source + count)
            for b in range(3)
        ]
        kernels = wg[pl.ds(low_tap * 3 * co, count * 3 * co), :]
        y = jnp.dot(jnp.concatenate(pieces, axis=1), kernels, preferred_element_type=F32)
        return narrow(y)

    def parted(p):
        inner = [a for a in range(3) if 1 <= p + a <= planes]
        return inner, [a for a in range(3) if a not in inner]

    def cells_at(p, row):
        return pl.ds(pl.multiple_of(p * plane + row, chunk), chunk)

    for copy in local[1:]:
        copy.wait()
    for side, (tap, source) in enumerate(((2, 0), (0, planes - 1))):

        def give(k, row, side=side, tap=tap, source=source):
            low = back_terms(0, row, tap, source, 1)
            high = back_terms(0, row + 2 * chunk, tap, source, 1)
            cs[side, pl.ds(row, chunk), :] = jnp.concatenate([low, high], axis=1).astype(BF16)

        chunks(give, 2)
    cot_halo[0]()

    for p in range(planes):

        def inner_first(k, row, p=p):
            hid[cells_at(p, row), :] = narrow(conv(pv, k1, p, k, parted(p)[0]))

        chunks(inner_first)

    for p in range(planes):

        def inner_back(k, row, p=p):
            inner = parted(p)[0]
            back[cells_at(p, row), :] = back_terms(p, row, inner[0], p + inner[0] - 1, len(inner))
            x = ct[p, pl.ds(pl.multiple_of(row + width, width), chunk), :].astype(F32)
            for c, y in enumerate((from_right(x), x, from_left(x))):
                ctt[pl.ds(c * co, co), cells_at(p, row)] = y.astype(BF16).T

        chunks(inner_back)

    volume_halo[1]()
    fill(pv, 0, ci)
    fill(pv, planes + 1, ci)

    for p in range(planes):

        def first_conv(k, row, p=p):
            at = cells_at(p, row)
            outer = parted(p)[1]
            hidden = hid[at, :]
            if outer:
                hidden = hidden + narrow(conv(pv, k1, p, k, outer))
            s = jax.nn.sigmoid(hidden)
            dsl[at, :] = s * (1.0 + hidden * (1.0 - s))
            place(pa, p + 1, k, (hidden * s).astype(BF16), cm)

        chunks(first_conv)
    act_halo[0]()

    cot_halo[1]()
    for p in range(planes):

        def grad_conv(k, row, p=p):
            at = cells_at(p, row)
            total = back[at, :]
            spot = pl.ds(pl.multiple_of(lax.rem(k, 2) * chunk, chunk), chunk)
            for side, own_plane in enumerate((0, planes - 1)):
                if p == own_plane:
                    x = cr[side, spot, :].astype(F32)
                    total = total + jnp.where(k < 2, x[:, :cm], x[:, cm:])
            rounded = (total * dsl[at, :]).astype(BF16)
            place(pg, p + 1, k, rounded, cm)
            x = rounded.astype(F32)
            spread = jnp.concatenate([from_right(x), x, from_left(x)], axis=1)
            ght[:, at] = spread.astype(BF16).T

        chunks(grad_conv)
    grad_halo[0]()

    def whole_window(ref, p):
        low = ref[p, pl.ds(0, half)].reshape(plane, ref.shape[4])
        high = ref[p, pl.ds(1, half)].reshape(plane, ref.shape[4])
        return jnp.concatenate([low, high], axis=1)

    def terms(acc, lhs, ref, a, ps):
        total = None
        for p in ps:
            term = jnp.dot(
                lhs[:, pl.ds(p * plane, plane)], whole_window(ref, p + a),
                preferred_element_type=F32,
            )
            total = term if total is None else total + term
        return total

    for a in range(3):
        acc1[a] = terms(acc1, ght, pv, a, range(planes))

    for p in range(planes):

        def inner_second(k, row, p=p):
            out[cells_at(p, row), :] = wide(conv(pa, k2, p, k, parted(p)[0]))

        chunks(inner_second)

    act_halo[1]()
    fill(pa, 0, cm)
    fill(pa, planes + 1, cm)

    for a in range(3):
        acc2[a] = terms(acc2, ctt, pa, a, range(planes))

    parity = lax.rem(me, 2)
    mine = me // 2
    used = 14 * (r1 + r2)
    for d in range(n):
        pieces = []
        for acc, r, c in ((acc2, r2, co), (acc1, r1, cm)):
            taps = [acc[t // 3, pl.ds(t % 3 * c + d * r, r), :] for t in range(9)]
            pieces += [x[:, : 2 * ci] for x in taps]
            last_taps = [x[:, 2 * ci : 3 * ci] for x in taps] + [jnp.zeros((r, ci), F32)]
            pieces += [
                jnp.concatenate(last_taps[2 * k : 2 * k + 2], axis=1) for k in range(5)
            ]
        if tx.shape[2] > used:
            pieces.append(jnp.zeros((tx.shape[2] - used, 2 * ci), F32))
        whole = jnp.concatenate(pieces, axis=0)
        own[d % 2, d // 2] = whole
        tx[d % 2, d // 2] = whole.astype(BF16)

    pair = pltpu.make_async_remote_copy(
        tx.at[1 - parity], rx, ps_sem.at[0], pr_sem.at[0],
        device_id={"space": me + 1 - 2 * parity}, device_id_type=MESH,
    )
    pair.start()

    stores = []
    for p in range(planes):

        def second_conv(k, row, p=p):
            outer = parted(p)[1]
            if outer:
                out[cells_at(p, row), :] += wide(conv(pa, k2, p, k, outer))

        chunks(second_conv)
        rows = pl.ds(p * plane, plane)
        stores.append(pltpu.make_async_copy(out.at[rows], out_hbm.at[rows], st_sem.at[p]))
        stores[-1].start()
    stores.append(pltpu.make_async_copy(gvol, gvol_hbm, st_sem.at[planes]))

    pair.wait_recv()

    def pair_sum(m, carry):
        ty[m] = (own[parity, m] + rx[m].astype(F32)).astype(BF16)
        return carry

    lax.fori_loop(0, n // 2, pair_sum, 0)
    sends = []
    for j in range(1, n // 2):
        slot = lax.rem(mine + j, n // 2)
        sends.append(
            pltpu.make_async_remote_copy(
                ty.at[slot], ry.at[j], ts_sem.at[j], tr_sem.at[j],
                device_id={"space": 2 * slot + parity}, device_id_type=MESH,
            )
        )
        sends[-1].start()

    for p in range(planes):

        def inner_last(k, row, p=p):
            gvol[cells_at(p, row), :] = narrow(conv(pg, k1f, p, k, parted(p)[0]))

        chunks(inner_last)

    grad_halo[1]()
    fill(pg, 0, cm)
    fill(pg, planes + 1, cm)

    for p in range(planes):

        def last_conv(k, row, p=p):
            outer = parted(p)[1]
            if outer:
                gvol[cells_at(p, row), :] += narrow(conv(pg, k1f, p, k, outer))

        chunks(last_conv)
    stores[-1].start()

    for send in sends:
        send.wait_recv()
    total = own[parity, mine] + rx[mine].astype(F32)
    for j in range(1, n // 2):
        total = total + ry[j].astype(F32)
    total = total * scale
    for t in range(14):
        if t < 9:
            taps = (t // 3 * 9 + t % 3, t // 3 * 9 + t % 3 + 3)
        else:
            taps = [u // 3 * 9 + u % 3 + 6 for u in (2 * (t - 9), 2 * (t - 9) + 1)]
        for side, tap in enumerate(taps):
            if tap < 27:
                lanes = slice(side * ci, (side + 1) * ci)
                g2[tap] = total[t * r2 : (t + 1) * r2, lanes]
                g1[tap] = total[14 * r2 + t * r1 : 14 * r2 + (t + 1) * r1, lanes]

    for store in stores:
        store.wait()
    pair.wait_send()
    for send in sends:
        send.wait_send()
    for exchange in (volume_halo, cot_halo, act_halo, grad_halo):
        exchange[2]()


def shards(volume, weight_one, weight_two, cotangent):
    n = lax.axis_size("space")
    planes, height, width, ci = volume.shape
    cm, co = weight_two.shape[3], weight_two.shape[4]
    plane = height * width
    cells = planes * plane
    pad = plane + 2 * width
    scale = 1.0 / math.sqrt(cells * n)

    w1 = weight_one.reshape(9, 3 * ci, cm)
    w2 = weight_two.reshape(9, 3 * cm, co)

    vmem = pl.BlockSpec(memory_space=pltpu.VMEM)
    hbm = pl.BlockSpec(memory_space=pltpu.HBM)
    rows = -(-14 * (cm // n + co // n) // 16) * 16
    out, gvol, g1, g2 = pl.pallas_call(
        functools.partial(kernel, n, planes, height, width, ci, cm, co, scale),
        out_shape=(
            jax.ShapeDtypeStruct((cells, co), F32),
            jax.ShapeDtypeStruct((cells, ci), F32),
            jax.ShapeDtypeStruct((27, cm // n, ci), F32),
            jax.ShapeDtypeStruct((27, co // n, cm), F32),
        ),
        in_specs=[hbm, hbm, hbm, hbm],
        out_specs=(hbm, hbm, vmem, vmem),
        scratch_shapes=[
            pltpu.VMEM((cells, co), F32),
            pltpu.VMEM((cells, ci), F32),
            pltpu.VMEM((planes + 2, height // 2 + 1, 2, width, 2 * ci), BF16),
            pltpu.VMEM((planes + 2, height // 2 + 1, 2, width, 2 * cm), BF16),
            pltpu.VMEM((planes + 2, height // 2 + 1, 2, width, 2 * cm), BF16),
            pltpu.VMEM((planes, pad, co), BF16),
            pltpu.VMEM((cells, ci), BF16),
            pltpu.VMEM((2, plane // 2, 2 * cm), BF16),
            pltpu.VMEM((2, plane // 2, 2 * cm), BF16),
            pltpu.VMEM((cells, cm), F32),
            pltpu.VMEM((cells, cm), F32),
            pltpu.VMEM((cells, cm), F32),
            pltpu.VMEM((3 * co, cells), BF16),
            pltpu.VMEM((3 * cm, cells), BF16),
            pltpu.VMEM((3, 3 * cm, 4 * ci), F32),
            pltpu.VMEM((3, 3 * co, 4 * cm), F32),
            pltpu.VMEM((9, 3 * ci, cm), BF16),
            pltpu.VMEM((9, 3 * cm, co), BF16),
            pltpu.VMEM((3, 4 * ci, 3 * cm), BF16),
            pltpu.VMEM((3, 4 * cm, 3 * ci), BF16),
            pltpu.VMEM((3, 4 * cm, 3 * co), BF16),
            pltpu.VMEM((9 * co, 3 * cm), BF16),
            pltpu.VMEM((2, n // 2, rows, 2 * ci), F32),
            pltpu.VMEM((2, n // 2, rows, 2 * ci), BF16),
            pltpu.VMEM((n // 2, rows, 2 * ci), BF16),
            pltpu.VMEM((n // 2, rows, 2 * ci), BF16),
            pltpu.VMEM((n // 2, rows, 2 * ci), BF16),
            pltpu.SemaphoreType.DMA((3 + planes,)),
            pltpu.SemaphoreType.DMA((planes + 1,)),
            pltpu.SemaphoreType.DMA((4, 2)),
            pltpu.SemaphoreType.DMA((4, 2)),
            pltpu.SemaphoreType.DMA((1,)),
            pltpu.SemaphoreType.DMA((1,)),
            pltpu.SemaphoreType.DMA((n // 2,)),
            pltpu.SemaphoreType.DMA((n // 2,)),
        ],
        compiler_params=pltpu.CompilerParams(
            collective_id=0, has_side_effects=True, vmem_limit_bytes=60 << 20
        ),
    )(
        volume.reshape(cells, ci), cotangent.reshape(cells, co), w1, w2
    )
    return (
        out.reshape(planes, height, width, co),
        gvol.reshape(planes, height, width, ci),
        jnp.transpose(g1.reshape(3, 3, 3, cm // n, ci), (0, 1, 2, 4, 3)),
        jnp.transpose(g2.reshape(3, 3, 3, co // n, cm), (0, 1, 2, 4, 3)),
    )


def solution(mesh):
    return jax.shard_map(
        shards,
        mesh=mesh,
        in_specs=(
            P(("groups", "space"), None, None, None),
            P(),
            P(),
            P(("groups", "space"), None, None, None),
        ),
        out_specs=(
            P(("groups", "space"), None, None, None),
            P(("groups", "space"), None, None, None),
            P("groups", None, None, None, "space"),
            P("groups", None, None, None, "space"),
        ),
        check_vma=False,
    )
```

```python
import functools
import math

import jax
import jax.numpy as jnp
from jax import lax
from jax.experimental import pallas as pl
from jax.experimental.pallas import tpu as pltpu
from jax.sharding import PartitionSpec as P

MESH = pl.DeviceIdType.MESH
F32 = jnp.float32
BF16 = jnp.bfloat16
TN = (((0,), (0,)), ((), ()))


def kernel(
    n, planes, height, width, ci, cm, co, scale,
    vol, cot, w1_in, w2_in,
    out_hbm, gvol_hbm, g1, g2,
    out, gvol, pv, pa, pg, ct, vraw, cs, cr, hid, dsl, back, ctt, ght, acc1, acc2,
    w1, w2, k1, k1f, k2, wg,
    tx1, rx1, ty1, ry1, own2, tx2, rx2, ty2, ry2,
    loc_sem, st_sem, hs_sem, hr_sem, ps_sem, pr_sem, ts_sem, tr_sem,
):
    me = lax.axis_index("space")
    plane = height * width
    chunk = plane // 4
    pad = plane + 2 * width
    half = height // 2
    step_rows = chunk // (2 * width)
    r1, r2 = cm // n, co // n

    barrier = pltpu.get_barrier_semaphore()
    for j in range(1, n):
        pl.semaphore_signal(
            barrier, inc=1, device_id={"space": lax.rem(me + j, n)}, device_id_type=MESH
        )

    local = [pltpu.make_async_copy(vol, vraw, loc_sem.at[0])]
    for p in range(planes):
        local.append(
            pltpu.make_async_copy(
                cot.at[pl.ds(p * plane, plane)],
                ct.at[p, pl.ds(width, plane)],
                loc_sem.at[1 + p],
            )
        )
    weights = [
        pltpu.make_async_copy(w2_in, w2, loc_sem.at[1 + planes]),
        pltpu.make_async_copy(w1_in, w1, loc_sem.at[2 + planes]),
    ]
    for copy in local[:1] + weights + local[1:]:
        copy.start()

    for ref in (pv, pa, pg):
        zero = jnp.zeros((width, ref.shape[4]), BF16)
        for p in range(planes + 2):
            ref[p, 0, 0] = zero
            ref[p, half, 0] = zero
            ref[p, half, 1] = zero
    zero = jnp.zeros((width, co), BF16)
    for p in range(planes):
        ct[p, pl.ds(0, width), :] = zero
        ct[p, pl.ds(pad - width, width), :] = zero

    def place(ref, p, k, x, c):
        m = k * step_rows
        x = x.reshape(step_rows, 2, width, c)
        ref[p, pl.ds(m, step_rows), :, :, c:] = x
        ref[p, pl.ds(m, step_rows), 1, :, :c] = x[:, 0]
        ref[p, pl.ds(m + 1, step_rows), 0, :, :c] = x[:, 1]

    def chunks(body, count=4):
        def step(k, carry):
            body(k, pl.multiple_of(k * chunk, chunk))
            return carry

        lax.fori_loop(0, count, step, 0, unroll=count)

    def fill(ref, p, c):
        x = ref[p, pl.ds(0, half), 1]
        ref[p, pl.ds(1, half), 0, :, :c] = x[:, :, c:]
        ref[p, pl.ds(0, half), 0, :, c:] = x[:, :, :c]

    local[0].wait()
    for p in range(planes):

        def own_volume(k, row, p=p):
            at = pl.ds(pl.multiple_of(p * plane + row, chunk), chunk)
            place(pv, p + 1, k, vraw[at, :], ci)

        chunks(own_volume)

    def halo(kind, low_src, high_src, low_dst, high_dst):
        left = pltpu.make_async_remote_copy(
            low_src, high_dst, hs_sem.at[kind, 0], hr_sem.at[kind, 0],
            device_id={"space": lax.rem(me + n - 1, n)}, device_id_type=MESH,
        )
        right = pltpu.make_async_remote_copy(
            high_src, low_dst, hs_sem.at[kind, 1], hr_sem.at[kind, 1],
            device_id={"space": lax.rem(me + 1, n)}, device_id_type=MESH,
        )

        def start():
            @pl.when(me > 0)
            def _():
                left.start()

            @pl.when(me < n - 1)
            def _():
                right.start()

        def wait_recv():
            @pl.when(me < n - 1)
            def _():
                left.wait_recv()

            @pl.when(me == n - 1)
            def _():
                high_dst[...] = jnp.zeros(high_dst.shape, BF16)

            @pl.when(me > 0)
            def _():
                right.wait_recv()

            @pl.when(me == 0)
            def _():
                low_dst[...] = jnp.zeros(low_dst.shape, BF16)

        def wait_send():
            @pl.when(me > 0)
            def _():
                left.wait_send()

            @pl.when(me < n - 1)
            def _():
                right.wait_send()

        return start, wait_recv, wait_send

    def field_halo(kind, ref):
        whole = pl.ds(0, half)
        return halo(
            kind,
            ref.at[1, whole, 1], ref.at[planes, whole, 1],
            ref.at[0, whole, 1], ref.at[planes + 1, whole, 1],
        )

    volume_halo = field_halo(0, pv)
    cot_halo = halo(1, cs.at[0], cs.at[1], cr.at[0], cr.at[1])
    act_halo = field_halo(2, pa)
    grad_halo = field_halo(3, pg)

    pl.semaphore_wait(barrier, n - 1)
    volume_halo[0]()

    for copy in weights:
        copy.wait()

    for t in range(9):
        w = w2[8 - t]
        order = [w[2 * cm :], w[:cm], w[cm : 2 * cm]]
        wg[pl.ds(t * co, co), :] = jnp.concatenate(order, axis=0).T
        a, b = t // 3, t % 3
        w = w1[8 - t]
        order = [w[2 * ci :], w[:ci], w[ci : 2 * ci]]
        k1f[a, pl.ds(b * cm, cm), :] = jnp.concatenate(order, axis=0).T
        w = w1[t]
        order = [w[:ci], w[2 * ci :], w[ci : 2 * ci]]
        k1[a, pl.ds(b * ci, ci), :] = jnp.concatenate(order, axis=1)
        w = w2[t]
        order = [w[:cm], w[cm : 2 * cm], w[2 * cm :]]
        k2[a, pl.ds(b * cm, cm), :] = jnp.concatenate(order, axis=1)
    for a in range(3):
        k1[a, pl.ds(3 * ci, ci), :] = jnp.zeros((ci, 3 * cm), BF16)
        k1f[a, pl.ds(3 * cm, cm), :] = jnp.zeros((cm, 3 * ci), BF16)
        k2[a, pl.ds(3 * cm, cm), :] = jnp.zeros((cm, 3 * co), BF16)

    column = lax.broadcasted_iota(jnp.int32, (chunk, 1), 0) % width
    first = column == 0
    last = column == width - 1
    low_lanes = lax.broadcasted_iota(jnp.int32, (1, 2 * cm), 1) < cm

    def from_left(x):
        return jnp.where(first, 0.0, pltpu.roll(x, 1, 0))

    def from_right(x):
        return jnp.where(last, 0.0, pltpu.roll(x, chunk - 1, 0))

    def narrow(y):
        c = y.shape[1] // 3
        z = y[:, : 2 * c]
        z = jnp.where(low_lanes, from_left(z), from_right(z))
        return z[:, :c] + z[:, c:] + y[:, 2 * c :]

    def wide(y):
        c = y.shape[1] // 3
        return from_left(y[:, :c]) + y[:, c : 2 * c] + from_right(y[:, 2 * c :])

    def window(ref, p, k):
        m = k * step_rows
        low = ref[p, pl.ds(m, step_rows)].reshape(chunk, ref.shape[4])
        high = ref[p, pl.ds(m + 1, step_rows)].reshape(chunk, ref.shape[4])
        return jnp.concatenate([low, high], axis=1)

    def conv(ref, kernels, p, k, taps):
        total = None
        for a in taps:
            term = jnp.dot(window(ref, p + a, k), kernels[a], preferred_element_type=F32)
            total = term if total is None else total + term
        return total

    def back_terms(p, row, low_tap, source, count):
        pieces = [
            ct[q, pl.ds(pl.multiple_of(row + b * width, width), chunk), :]
            for q in range(source, source + count)
            for b in range(3)
        ]
        kernels = wg[pl.ds(low_tap * 3 * co, count * 3 * co), :]
        y = jnp.dot(jnp.concatenate(pieces, axis=1), kernels, preferred_element_type=F32)
        return narrow(y)

    def parted(p):
        inner = [a for a in range(3) if 1 <= p + a <= planes]
        return inner, [a for a in range(3) if a not in inner]

    def cells_at(p, row):
        return pl.ds(pl.multiple_of(p * plane + row, chunk), chunk)

    for copy in local[1:]:
        copy.wait()
    for side, (tap, source) in enumerate(((2, 0), (0, planes - 1))):

        def give(k, row, side=side, tap=tap, source=source):
            low = back_terms(0, row, tap, source, 1)
            high = back_terms(0, row + 2 * chunk, tap, source, 1)
            cs[side, pl.ds(row, chunk), :] = jnp.concatenate([low, high], axis=1).astype(BF16)

        chunks(give, 2)

    for p in range(planes):

        def inner_first(k, row, p=p):
            hid[cells_at(p, row), :] = narrow(conv(pv, k1, p, k, parted(p)[0]))

        chunks(inner_first)

    for p in range(planes):

        def inner_back(k, row, p=p):
            inner = parted(p)[0]
            back[cells_at(p, row), :] = back_terms(p, row, inner[0], p + inner[0] - 1, len(inner))
            x = ct[p, pl.ds(pl.multiple_of(row + width, width), chunk), :].astype(F32)
            for c, y in enumerate((from_right(x), x, from_left(x))):
                ctt[pl.ds(c * co, co), cells_at(p, row)] = y.astype(BF16).T

        chunks(inner_back)

    volume_halo[1]()
    cot_halo[0]()
    fill(pv, 0, ci)
    fill(pv, planes + 1, ci)

    for p in range(planes):

        def first_conv(k, row, p=p):
            at = cells_at(p, row)
            outer = parted(p)[1]
            hidden = hid[at, :]
            if outer:
                hidden = hidden + narrow(conv(pv, k1, p, k, outer))
            s = jax.nn.sigmoid(hidden)
            dsl[at, :] = s * (1.0 + hidden * (1.0 - s))
            place(pa, p + 1, k, (hidden * s).astype(BF16), cm)

        chunks(first_conv)
    act_halo[0]()

    def whole_window(ref, p):
        low = ref[p, pl.ds(0, half)].reshape(plane, ref.shape[4])
        high = ref[p, pl.ds(1, half)].reshape(plane, ref.shape[4])
        return jnp.concatenate([low, high], axis=1)

    def terms(acc, lhs, ref, a, ps):
        total = None
        for p in ps:
            term = jnp.dot(
                lhs[:, pl.ds(p * plane, plane)], whole_window(ref, p + a),
                preferred_element_type=F32,
            )
            total = term if total is None else total + term
        return total

    parity = lax.rem(me, 2)
    mine = me // 2

    def scatter(kind, acc, c, r, own, tx, rx, ty, ry):
        used = 14 * r

        def pack():
            for d in range(n):
                taps = [acc[t // 3, pl.ds(t % 3 * c + d * r, r), :] for t in range(9)]
                pieces = [x[:, : 2 * ci] for x in taps]
                last_taps = [x[:, 2 * ci : 3 * ci] for x in taps] + [jnp.zeros((r, ci), F32)]
                pieces += [
                    jnp.concatenate(last_taps[2 * k : 2 * k + 2], axis=1) for k in range(5)
                ]
                if tx.shape[2] > used:
                    pieces.append(jnp.zeros((tx.shape[2] - used, 2 * ci), F32))
                whole = jnp.concatenate(pieces, axis=0)
                if own is not tx:
                    own[d % 2, d // 2] = whole
                tx[d % 2, d // 2] = whole.astype(tx.dtype)

        pair = pltpu.make_async_remote_copy(
            tx.at[1 - parity], rx, ps_sem.at[kind], pr_sem.at[kind],
            device_id={"space": me + 1 - 2 * parity}, device_id_type=MESH,
        )
        sends = []
        for j in range(1, n // 2):
            slot = lax.rem(mine + j, n // 2)
            sends.append(
                pltpu.make_async_remote_copy(
                    ty.at[slot], ry.at[j], ts_sem.at[kind, j], tr_sem.at[kind, j],
                    device_id={"space": 2 * slot + parity}, device_id_type=MESH,
                )
            )

        def start():
            pack()
            pair.start()

        def forward():
            pair.wait_recv()

            def pair_sum(m, carry):
                ty[m] = (own[parity, m] + rx[m].astype(F32)).astype(BF16)
                return carry

            lax.fori_loop(0, n // 2, pair_sum, 0)
            for send in sends:
                send.start()

        def finish(result):
            for send in sends:
                send.wait_recv()
            total = own[parity, mine] + rx[mine].astype(F32)
            for j in range(1, n // 2):
                total = total + ry[j].astype(F32)
            total = total * scale
            for t in range(14):
                if t < 9:
                    taps = (t // 3 * 9 + t % 3, t // 3 * 9 + t % 3 + 3)
                else:
                    taps = [u // 3 * 9 + u % 3 + 6 for u in (2 * (t - 9), 2 * (t - 9) + 1)]
                for side, tap in enumerate(taps):
                    if tap < 27:
                        lanes = slice(side * ci, (side + 1) * ci)
                        result[tap] = total[t * r : (t + 1) * r, lanes]

        def wait_send():
            pair.wait_send()
            for send in sends:
                send.wait_send()

        return start, forward, finish, wait_send

    first_sum = scatter(0, acc1, cm, r1, tx1, tx1, rx1, ty1, ry1)
    second_sum = scatter(1, acc2, co, r2, own2, tx2, rx2, ty2, ry2)

    def by_place(a, inside):
        return [p for p in range(planes) if (1 <= p + a <= planes) == inside]

    for a in range(3):
        acc2[a] = terms(acc2, ctt, pa, a, by_place(a, True))

    for p in range(planes):

        def inner_second(k, row, p=p):
            out[cells_at(p, row), :] = wide(conv(pa, k2, p, k, parted(p)[0]))

        chunks(inner_second)

    cot_halo[1]()
    for p in range(planes):

        def grad_conv(k, row, p=p):
            at = cells_at(p, row)
            total = back[at, :]
            spot = pl.ds(pl.multiple_of(lax.rem(k, 2) * chunk, chunk), chunk)
            for side, own_plane in enumerate((0, planes - 1)):
                if p == own_plane:
                    x = cr[side, spot, :].astype(F32)
                    total = total + jnp.where(k < 2, x[:, :cm], x[:, cm:])
            rounded = (total * dsl[at, :]).astype(BF16)
            place(pg, p + 1, k, rounded, cm)
            x = rounded.astype(F32)
            spread = jnp.concatenate([from_right(x), x, from_left(x)], axis=1)
            ght[:, at] = spread.astype(BF16).T

        chunks(grad_conv)
    grad_halo[0]()

    for a in range(3):
        acc1[a] = terms(acc1, ght, pv, a, range(planes))
    first_sum[0]()

    act_halo[1]()
    fill(pa, 0, cm)
    fill(pa, planes + 1, cm)

    for a in range(3):
        outer = by_place(a, False)
        if outer:
            acc2[a] += terms(acc2, ctt, pa, a, outer)
    second_sum[0]()
    first_sum[1]()

    stores = []
    for p in range(planes):

        def second_conv(k, row, p=p):
            outer = parted(p)[1]
            if outer:
                out[cells_at(p, row), :] += wide(conv(pa, k2, p, k, outer))

        chunks(second_conv)
        rows = pl.ds(p * plane, plane)
        stores.append(pltpu.make_async_copy(out.at[rows], out_hbm.at[rows], st_sem.at[p]))
        stores[-1].start()
    stores.append(pltpu.make_async_copy(gvol, gvol_hbm, st_sem.at[planes]))

    second_sum[1]()

    for p in range(planes):

        def inner_last(k, row, p=p):
            gvol[cells_at(p, row), :] = narrow(conv(pg, k1f, p, k, parted(p)[0]))

        chunks(inner_last)


    grad_halo[1]()
    fill(pg, 0, cm)
    fill(pg, planes + 1, cm)

    for p in range(planes):

        def last_conv(k, row, p=p):
            outer = parted(p)[1]
            if outer:
                gvol[cells_at(p, row), :] += narrow(conv(pg, k1f, p, k, outer))

        chunks(last_conv)
    stores[-1].start()

    first_sum[2](g1)
    second_sum[2](g2)

    for store in stores:
        store.wait()
    for exchange in (first_sum, second_sum):
        exchange[3]()
    for exchange in (volume_halo, cot_halo, act_halo, grad_halo):
        exchange[2]()


def hand_over(parts, *refs):
    count = len(parts)
    sources, targets, held = (refs[k * count : (k + 1) * count] for k in range(3))
    in_sem, out_sem = refs[3 * count :]
    copies = []
    for source, target, kept, cuts in zip(sources, targets, held, parts):
        rows = source.shape[0] // cuts
        for k in range(cuts):
            piece = pl.ds(k * rows, rows)
            at = len(copies)
            copies.append((
                pltpu.make_async_copy(source.at[piece], kept.at[piece], in_sem.at[at]),
                pltpu.make_async_copy(kept.at[piece], target.at[piece], out_sem.at[at]),
            ))
            copies[-1][0].start()
    for load, store in copies:
        load.wait()
        store.start()
    for load, store in copies:
        store.wait()


def shards(volume, weight_one, weight_two, cotangent):
    n = lax.axis_size("space")
    planes, height, width, ci = volume.shape
    cm, co = weight_two.shape[3], weight_two.shape[4]
    plane = height * width
    cells = planes * plane
    pad = plane + 2 * width
    scale = 1.0 / math.sqrt(cells * n)

    w1 = weight_one.reshape(9, 3 * ci, cm)
    w2 = weight_two.reshape(9, 3 * cm, co)

    vmem = pl.BlockSpec(memory_space=pltpu.VMEM)
    hbm = pl.BlockSpec(memory_space=pltpu.HBM)
    rows1, rows2 = (-(-14 * (c // n) // 16) * 16 for c in (cm, co))
    out, gvol, g1, g2 = pl.pallas_call(
        functools.partial(kernel, n, planes, height, width, ci, cm, co, scale),
        out_shape=(
            jax.ShapeDtypeStruct((cells, co), F32),
            jax.ShapeDtypeStruct((cells, ci), F32),
            jax.ShapeDtypeStruct((27, cm // n, ci), F32),
            jax.ShapeDtypeStruct((27, co // n, cm), F32),
        ),
        in_specs=[hbm, hbm, hbm, hbm],
        out_specs=(hbm, hbm, vmem, vmem),
        scratch_shapes=[
            pltpu.VMEM((cells, co), F32),
            pltpu.VMEM((cells, ci), F32),
            pltpu.VMEM((planes + 2, height // 2 + 1, 2, width, 2 * ci), BF16),
            pltpu.VMEM((planes + 2, height // 2 + 1, 2, width, 2 * cm), BF16),
            pltpu.VMEM((planes + 2, height // 2 + 1, 2, width, 2 * cm), BF16),
            pltpu.VMEM((planes, pad, co), BF16),
            pltpu.VMEM((cells, ci), BF16),
            pltpu.VMEM((2, plane // 2, 2 * cm), BF16),
            pltpu.VMEM((2, plane // 2, 2 * cm), BF16),
            pltpu.VMEM((cells, cm), F32),
            pltpu.VMEM((cells, cm), F32),
            pltpu.VMEM((cells, cm), F32),
            pltpu.VMEM((3 * co, cells), BF16),
            pltpu.VMEM((3 * cm, cells), BF16),
            pltpu.VMEM((3, 3 * cm, 4 * ci), F32),
            pltpu.VMEM((3, 3 * co, 4 * cm), F32),
            pltpu.VMEM((9, 3 * ci, cm), BF16),
            pltpu.VMEM((9, 3 * cm, co), BF16),
            pltpu.VMEM((3, 4 * ci, 3 * cm), BF16),
            pltpu.VMEM((3, 4 * cm, 3 * ci), BF16),
            pltpu.VMEM((3, 4 * cm, 3 * co), BF16),
            pltpu.VMEM((9 * co, 3 * cm), BF16),
            pltpu.VMEM((2, n // 2, rows1, 2 * ci), F32),
            pltpu.VMEM((n // 2, rows1, 2 * ci), F32),
            pltpu.VMEM((n // 2, rows1, 2 * ci), BF16),
            pltpu.VMEM((n // 2, rows1, 2 * ci), BF16),
            pltpu.VMEM((2, n // 2, rows2, 2 * ci), F32),
            pltpu.VMEM((2, n // 2, rows2, 2 * ci), BF16),
            pltpu.VMEM((n // 2, rows2, 2 * ci), BF16),
            pltpu.VMEM((n // 2, rows2, 2 * ci), BF16),
            pltpu.VMEM((n // 2, rows2, 2 * ci), BF16),
            pltpu.SemaphoreType.DMA((3 + planes,)),
            pltpu.SemaphoreType.DMA((planes + 1,)),
            pltpu.SemaphoreType.DMA((4, 2)),
            pltpu.SemaphoreType.DMA((4, 2)),
            pltpu.SemaphoreType.DMA((2,)),
            pltpu.SemaphoreType.DMA((2,)),
            pltpu.SemaphoreType.DMA((2, n // 2)),
            pltpu.SemaphoreType.DMA((2, n // 2)),
        ],
        compiler_params=pltpu.CompilerParams(
            collective_id=0, has_side_effects=True, vmem_limit_bytes=60 << 20
        ),
    )(
        volume.reshape(cells, ci), cotangent.reshape(cells, co), w1, w2
    )
    results = (out, gvol, g1, g2)
    parts = (4, 4, 1, 1)
    out, gvol, g1, g2 = pl.pallas_call(
        functools.partial(hand_over, parts),
        out_shape=tuple(jax.ShapeDtypeStruct(x.shape, x.dtype) for x in results),
        in_specs=[hbm] * 4,
        out_specs=(hbm,) * 4,
        scratch_shapes=[pltpu.VMEM(x.shape, x.dtype) for x in results]
        + [pltpu.SemaphoreType.DMA((sum(parts),))] * 2,
        compiler_params=pltpu.CompilerParams(vmem_limit_bytes=60 << 20),
    )(*results)
    return (
        out.reshape(planes, height, width, co),
        gvol.reshape(planes, height, width, ci),
        jnp.transpose(g1.reshape(3, 3, 3, cm // n, ci), (0, 1, 2, 4, 3)),
        jnp.transpose(g2.reshape(3, 3, 3, co // n, cm), (0, 1, 2, 4, 3)),
    )


def solution(mesh):
    return jax.shard_map(
        shards,
        mesh=mesh,
        in_specs=(
            P(("groups", "space"), None, None, None),
            P(),
            P(),
            P(("groups", "space"), None, None, None),
        ),
        out_specs=(
            P(("groups", "space"), None, None, None),
            P(("groups", "space"), None, None, None),
            P("groups", None, None, None, "space"),
            P("groups", None, None, None, "space"),
        ),
        check_vma=False,
    )
```

```python
import functools
import math

import jax
import jax.numpy as jnp
from jax import lax
from jax.experimental import pallas as pl
from jax.experimental.pallas import tpu as pltpu
from jax.sharding import PartitionSpec as P

MESH = pl.DeviceIdType.MESH
F32 = jnp.float32
BF16 = jnp.bfloat16
TN = (((0,), (0,)), ((), ()))


def kernel(
    n, planes, height, width, ci, cm, co, scale,
    vol, cot, w1_in, w2_in,
    out_hbm, gvol_hbm, g1, g2,
    out, gvol, pv, pa, pg, ct, vraw, cs, cr, hid, dsl, back, ctt, ght, acc1, acc2,
    w1, w2, k1, k1f, k2, wg,
    tx1, rx1, ty1, ry1, own2, tx2, rx2, ty2, ry2,
    loc_sem, st_sem, hs_sem, hr_sem, ps_sem, pr_sem, ts_sem, tr_sem,
):
    me = lax.axis_index("space")
    plane = height * width
    chunk = plane // 4
    pad = plane + 2 * width
    half = height // 2
    step_rows = chunk // (2 * width)
    r1, r2 = cm // n, co // n

    barrier = pltpu.get_barrier_semaphore()
    for j in range(1, n):
        pl.semaphore_signal(
            barrier, inc=1, device_id={"space": lax.rem(me + j, n)}, device_id_type=MESH
        )

    local = [pltpu.make_async_copy(vol, vraw, loc_sem.at[0])]
    for p in range(planes):
        local.append(
            pltpu.make_async_copy(
                cot.at[pl.ds(p * plane, plane)],
                ct.at[p, pl.ds(width, plane)],
                loc_sem.at[1 + p],
            )
        )
    weights = [
        pltpu.make_async_copy(w2_in, w2, loc_sem.at[1 + planes]),
        pltpu.make_async_copy(w1_in, w1, loc_sem.at[2 + planes]),
    ]
    for copy in local[:1] + weights + local[1:]:
        copy.start()

    for ref in (pv, pa, pg):
        zero = jnp.zeros((width, ref.shape[4]), BF16)
        for p in range(planes + 2):
            ref[p, 0, 0] = zero
            ref[p, half, 0] = zero
            ref[p, half, 1] = zero
    zero = jnp.zeros((width, co), BF16)
    for p in range(planes):
        ct[p, pl.ds(0, width), :] = zero
        ct[p, pl.ds(pad - width, width), :] = zero

    def place(ref, p, k, x, c):
        m = k * step_rows
        x = x.reshape(step_rows, 2, width, c)
        ref[p, pl.ds(m, step_rows), :, :, c:] = x
        ref[p, pl.ds(m, step_rows), 1, :, :c] = x[:, 0]
        ref[p, pl.ds(m + 1, step_rows), 0, :, :c] = x[:, 1]

    def chunks(body, count=4):
        def step(k, carry):
            body(k, pl.multiple_of(k * chunk, chunk))
            return carry

        lax.fori_loop(0, count, step, 0, unroll=count)

    def fill(ref, p, c):
        x = ref[p, pl.ds(0, half), 1]
        ref[p, pl.ds(1, half), 0, :, :c] = x[:, :, c:]
        ref[p, pl.ds(0, half), 0, :, c:] = x[:, :, :c]

    local[0].wait()
    for p in range(planes):

        def own_volume(k, row, p=p):
            at = pl.ds(pl.multiple_of(p * plane + row, chunk), chunk)
            place(pv, p + 1, k, vraw[at, :], ci)

        chunks(own_volume)

    def halo(kind, low_src, high_src, low_dst, high_dst):
        left = pltpu.make_async_remote_copy(
            low_src, high_dst, hs_sem.at[kind, 0], hr_sem.at[kind, 0],
            device_id={"space": lax.rem(me + n - 1, n)}, device_id_type=MESH,
        )
        right = pltpu.make_async_remote_copy(
            high_src, low_dst, hs_sem.at[kind, 1], hr_sem.at[kind, 1],
            device_id={"space": lax.rem(me + 1, n)}, device_id_type=MESH,
        )

        def start():
            @pl.when(me > 0)
            def _():
                left.start()

            @pl.when(me < n - 1)
            def _():
                right.start()

        def wait_recv():
            @pl.when(me < n - 1)
            def _():
                left.wait_recv()

            @pl.when(me == n - 1)
            def _():
                high_dst[...] = jnp.zeros(high_dst.shape, BF16)

            @pl.when(me > 0)
            def _():
                right.wait_recv()

            @pl.when(me == 0)
            def _():
                low_dst[...] = jnp.zeros(low_dst.shape, BF16)

        def wait_send():
            @pl.when(me > 0)
            def _():
                left.wait_send()

            @pl.when(me < n - 1)
            def _():
                right.wait_send()

        return start, wait_recv, wait_send

    def field_halo(kind, ref):
        whole = pl.ds(0, half)
        return halo(
            kind,
            ref.at[1, whole, 1], ref.at[planes, whole, 1],
            ref.at[0, whole, 1], ref.at[planes + 1, whole, 1],
        )

    volume_halo = field_halo(0, pv)
    cot_halo = halo(1, cs.at[0], cs.at[1], cr.at[0], cr.at[1])
    act_halo = field_halo(2, pa)
    grad_halo = field_halo(3, pg)

    pl.semaphore_wait(barrier, n - 1)
    volume_halo[0]()

    for copy in weights:
        copy.wait()

    for t in range(9):
        w = w2[8 - t]
        order = [w[2 * cm :], w[:cm], w[cm : 2 * cm]]
        wg[pl.ds(t * co, co), :] = jnp.concatenate(order, axis=0).T
        a, b = t // 3, t % 3
        w = w1[8 - t]
        order = [w[2 * ci :], w[:ci], w[ci : 2 * ci]]
        k1f[a, pl.ds(b * cm, cm), :] = jnp.concatenate(order, axis=0).T
        w = w1[t]
        order = [w[:ci], w[2 * ci :], w[ci : 2 * ci]]
        k1[a, pl.ds(b * ci, ci), :] = jnp.concatenate(order, axis=1)
        w = w2[t]
        order = [w[:cm], w[cm : 2 * cm], w[2 * cm :]]
        k2[a, pl.ds(b * cm, cm), :] = jnp.concatenate(order, axis=1)
    for a in range(3):
        k1[a, pl.ds(3 * ci, ci), :] = jnp.zeros((ci, 3 * cm), BF16)
        k1f[a, pl.ds(3 * cm, cm), :] = jnp.zeros((cm, 3 * ci), BF16)
        k2[a, pl.ds(3 * cm, cm), :] = jnp.zeros((cm, 3 * co), BF16)

    column = lax.broadcasted_iota(jnp.int32, (chunk, 1), 0) % width
    first = column == 0
    last = column == width - 1
    low_lanes = lax.broadcasted_iota(jnp.int32, (1, 2 * cm), 1) < cm

    def from_left(x):
        return jnp.where(first, 0.0, pltpu.roll(x, 1, 0))

    def from_right(x):
        return jnp.where(last, 0.0, pltpu.roll(x, chunk - 1, 0))

    def narrow(y):
        c = y.shape[1] // 3
        z = y[:, : 2 * c]
        z = jnp.where(low_lanes, from_left(z), from_right(z))
        return z[:, :c] + z[:, c:] + y[:, 2 * c :]

    def wide(y):
        c = y.shape[1] // 3
        return from_left(y[:, :c]) + y[:, c : 2 * c] + from_right(y[:, 2 * c :])

    def window(ref, p, k):
        m = k * step_rows
        low = ref[p, pl.ds(m, step_rows)].reshape(chunk, ref.shape[4])
        high = ref[p, pl.ds(m + 1, step_rows)].reshape(chunk, ref.shape[4])
        return jnp.concatenate([low, high], axis=1)

    def conv(ref, kernels, p, k, taps):
        total = None
        for a in taps:
            term = jnp.dot(window(ref, p + a, k), kernels[a], preferred_element_type=F32)
            total = term if total is None else total + term
        return total

    def back_terms(p, row, low_tap, source, count):
        pieces = [
            ct[q, pl.ds(pl.multiple_of(row + b * width, width), chunk), :]
            for q in range(source, source + count)
            for b in range(3)
        ]
        kernels = wg[pl.ds(low_tap * 3 * co, count * 3 * co), :]
        y = jnp.dot(jnp.concatenate(pieces, axis=1), kernels, preferred_element_type=F32)
        return narrow(y)

    def parted(p):
        inner = [a for a in range(3) if 1 <= p + a <= planes]
        return inner, [a for a in range(3) if a not in inner]

    def cells_at(p, row):
        return pl.ds(pl.multiple_of(p * plane + row, chunk), chunk)

    for copy in local[1:]:
        copy.wait()
    for side, (tap, source) in enumerate(((2, 0), (0, planes - 1))):

        def give(k, row, side=side, tap=tap, source=source):
            low = back_terms(0, row, tap, source, 1)
            high = back_terms(0, row + 2 * chunk, tap, source, 1)
            cs[side, pl.ds(row, chunk), :] = jnp.concatenate([low, high], axis=1).astype(BF16)

        chunks(give, 2)

    for p in range(planes):

        def inner_first(k, row, p=p):
            hid[cells_at(p, row), :] = narrow(conv(pv, k1, p, k, parted(p)[0]))

        chunks(inner_first)

    for p in range(planes):

        def inner_back(k, row, p=p):
            inner = parted(p)[0]
            back[cells_at(p, row), :] = back_terms(p, row, inner[0], p + inner[0] - 1, len(inner))
            x = ct[p, pl.ds(pl.multiple_of(row + width, width), chunk), :].astype(F32)
            for c, y in enumerate((from_right(x), x, from_left(x))):
                ctt[pl.ds(c * co, co), cells_at(p, row)] = y.astype(BF16).T

        chunks(inner_back)

    volume_halo[1]()
    cot_halo[0]()
    fill(pv, 0, ci)
    fill(pv, planes + 1, ci)

    for p in range(planes):

        def first_conv(k, row, p=p):
            at = cells_at(p, row)
            outer = parted(p)[1]
            hidden = hid[at, :]
            if outer:
                hidden = hidden + narrow(conv(pv, k1, p, k, outer))
            s = jax.nn.sigmoid(hidden)
            dsl[at, :] = s * (1.0 + hidden * (1.0 - s))
            place(pa, p + 1, k, (hidden * s).astype(BF16), cm)

        chunks(first_conv)
    act_halo[0]()

    def whole_window(ref, p):
        low = ref[p, pl.ds(0, half)].reshape(plane, ref.shape[4])
        high = ref[p, pl.ds(1, half)].reshape(plane, ref.shape[4])
        return jnp.concatenate([low, high], axis=1)

    def terms(acc, lhs, ref, a, ps):
        total = None
        for p in ps:
            term = jnp.dot(
                lhs[:, pl.ds(p * plane, plane)], whole_window(ref, p + a),
                preferred_element_type=F32,
            )
            total = term if total is None else total + term
        return total

    parity = lax.rem(me, 2)
    mine = me // 2

    def scatter(kind, groups, own, tx, rx, ty, ry):
        def pack():
            for d in range(n):
                pieces = []
                for acc, c, r, taps, _ in groups:
                    blocks = [acc[a, pl.ds(t * c + d * r, r), :] for a, t in taps]
                    pieces += [x[:, : 2 * ci] for x in blocks]
                    tails = [x[:, 2 * ci : 3 * ci] for x in blocks]
                    if len(tails) % 2:
                        tails.append(jnp.zeros((r, ci), F32))
                    pieces += [
                        jnp.concatenate(tails[k : k + 2], axis=1) for k in range(0, len(tails), 2)
                    ]
                used = sum(x.shape[0] for x in pieces)
                if tx.shape[2] > used:
                    pieces.append(jnp.zeros((tx.shape[2] - used, 2 * ci), F32))
                whole = jnp.concatenate(pieces, axis=0)
                if own is not tx:
                    own[d % 2, d // 2] = whole
                tx[d % 2, d // 2] = whole.astype(tx.dtype)

        pair = pltpu.make_async_remote_copy(
            tx.at[1 - parity], rx, ps_sem.at[kind], pr_sem.at[kind],
            device_id={"space": me + 1 - 2 * parity}, device_id_type=MESH,
        )
        sends = []
        for j in range(1, n // 2):
            slot = lax.rem(mine + j, n // 2)
            sends.append(
                pltpu.make_async_remote_copy(
                    ty.at[slot], ry.at[j], ts_sem.at[kind, j], tr_sem.at[kind, j],
                    device_id={"space": 2 * slot + parity}, device_id_type=MESH,
                )
            )

        def start():
            pack()
            pair.start()

        def forward():
            pair.wait_recv()

            def pair_sum(m, carry):
                ty[m] = (own[parity, m] + rx[m].astype(F32)).astype(BF16)
                return carry

            lax.fori_loop(0, n // 2, pair_sum, 0)
            for send in sends:
                send.start()

        def finish():
            for send in sends:
                send.wait_recv()
            total = own[parity, mine] + rx[mine].astype(F32)
            for j in range(1, n // 2):
                total = total + ry[j].astype(F32)
            total = total * scale
            at = 0
            for _, _, r, taps, result in groups:
                after = at + len(taps) * r
                for k, (a, t) in enumerate(taps):
                    low = at + k * r
                    result[a * 9 + t] = total[low : low + r, :ci]
                    result[a * 9 + 3 + t] = total[low : low + r, ci:]
                    low, lanes = after + k // 2 * r, k % 2 * ci
                    result[a * 9 + 6 + t] = total[low : low + r, lanes : lanes + ci]
                at = after + -(-len(taps) // 2) * r

        def wait_send():
            pair.wait_send()
            for send in sends:
                send.wait_send()

        return start, forward, finish, wait_send

    def taps_of(*depth_taps):
        return [(a, t) for a in depth_taps for t in range(3)]

    first_sum = scatter(
        0, [(acc2, co, r2, taps_of(1), g2), (acc1, cm, r1, taps_of(0, 1, 2), g1)],
        tx1, tx1, rx1, ty1, ry1,
    )
    second_sum = scatter(1, [(acc2, co, r2, taps_of(0, 2), g2)], own2, tx2, rx2, ty2, ry2)

    def by_place(a, inside):
        return [p for p in range(planes) if (1 <= p + a <= planes) == inside]

    for a in range(3):
        acc2[a] = terms(acc2, ctt, pa, a, by_place(a, True))

    for p in range(planes):

        def inner_second(k, row, p=p):
            out[cells_at(p, row), :] = wide(conv(pa, k2, p, k, parted(p)[0]))

        chunks(inner_second)

    cot_halo[1]()
    for p in range(planes):

        def grad_conv(k, row, p=p):
            at = cells_at(p, row)
            total = back[at, :]
            spot = pl.ds(pl.multiple_of(lax.rem(k, 2) * chunk, chunk), chunk)
            for side, own_plane in enumerate((0, planes - 1)):
                if p == own_plane:
                    x = cr[side, spot, :].astype(F32)
                    total = total + jnp.where(k < 2, x[:, :cm], x[:, cm:])
            rounded = (total * dsl[at, :]).astype(BF16)
            place(pg, p + 1, k, rounded, cm)
            x = rounded.astype(F32)
            spread = jnp.concatenate([from_right(x), x, from_left(x)], axis=1)
            ght[:, at] = spread.astype(BF16).T

        chunks(grad_conv)
    grad_halo[0]()

    for a in range(3):
        acc1[a] = terms(acc1, ght, pv, a, range(planes))
    first_sum[0]()

    act_halo[1]()
    fill(pa, 0, cm)
    fill(pa, planes + 1, cm)

    for a in range(3):
        outer = by_place(a, False)
        if outer:
            acc2[a] += terms(acc2, ctt, pa, a, outer)
    second_sum[0]()
    first_sum[1]()

    stores = []
    for p in range(planes):

        def second_conv(k, row, p=p):
            outer = parted(p)[1]
            if outer:
                out[cells_at(p, row), :] += wide(conv(pa, k2, p, k, outer))

        chunks(second_conv)
        rows = pl.ds(p * plane, plane)
        stores.append(pltpu.make_async_copy(out.at[rows], out_hbm.at[rows], st_sem.at[p]))
        stores[-1].start()
    stores.append(pltpu.make_async_copy(gvol, gvol_hbm, st_sem.at[planes]))

    second_sum[1]()

    def pair_at(p, row):
        side = 2 * p // planes
        return cells_at(p - side * (planes // 2), row), slice(side * ci, (side + 1) * ci)

    for p in range(planes):

        def inner_last(k, row, p=p):
            gvol[pair_at(p, row)] = narrow(conv(pg, k1f, p, k, parted(p)[0]))

        chunks(inner_last)


    grad_halo[1]()
    fill(pg, 0, cm)
    fill(pg, planes + 1, cm)

    for p in range(planes):

        def last_conv(k, row, p=p):
            outer = parted(p)[1]
            if outer:
                gvol[pair_at(p, row)] += narrow(conv(pg, k1f, p, k, outer))

        chunks(last_conv)
    stores[-1].start()

    first_sum[2]()
    second_sum[2]()

    for store in stores:
        store.wait()
    for exchange in (first_sum, second_sum):
        exchange[3]()
    for exchange in (volume_halo, cot_halo, act_halo, grad_halo):
        exchange[2]()


def hand_over(
    out, gvol, g1, g2, out_to, gvol_to, g1_to, g2_to,
    out_kept, pairs, gvol_kept, g1_kept, g2_kept, in_sem, out_sem,
):
    cuts = 4
    loads, stores = [], []

    def load(source, kept):
        loads.append(pltpu.make_async_copy(source, kept, in_sem.at[len(loads)]))
        loads[-1].start()

    def store(kept, target):
        stores.append(pltpu.make_async_copy(kept, target, out_sem.at[len(stores)]))
        stores[-1].start()

    def pieces(ref):
        rows = ref.shape[0] // cuts
        return [pl.ds(k * rows, rows) for k in range(cuts)]

    for piece in pieces(pairs):
        load(gvol.at[piece], pairs.at[piece])
    load(g1, g1_kept)
    load(g2, g2_kept)
    for piece in pieces(out):
        load(out.at[piece], out_kept.at[piece])
    half, width = pairs.shape[0], gvol_kept.shape[1]
    for k, piece in enumerate(pieces(pairs)):
        loads[k].wait()
        x = pairs[piece, :]
        for side in range(2):
            spot = pl.ds(side * half + k * (half // cuts), half // cuts)
            gvol_kept[spot, :] = x[:, side * width : (side + 1) * width]
            store(gvol_kept.at[spot], gvol_to.at[spot])
    loads[cuts].wait()
    store(g1_kept, g1_to)
    loads[cuts + 1].wait()
    store(g2_kept, g2_to)
    for k, piece in enumerate(pieces(out)):
        loads[cuts + 2 + k].wait()
        store(out_kept.at[piece], out_to.at[piece])
    for copy in stores:
        copy.wait()


def shards(volume, weight_one, weight_two, cotangent):
    n = lax.axis_size("space")
    planes, height, width, ci = volume.shape
    cm, co = weight_two.shape[3], weight_two.shape[4]
    plane = height * width
    cells = planes * plane
    pad = plane + 2 * width
    scale = 1.0 / math.sqrt(cells * n)

    w1 = weight_one.reshape(9, 3 * ci, cm)
    w2 = weight_two.reshape(9, 3 * cm, co)

    vmem = pl.BlockSpec(memory_space=pltpu.VMEM)
    hbm = pl.BlockSpec(memory_space=pltpu.HBM)
    rows1, rows2 = (-(-x // n // 16) * 16 for x in (14 * cm + 5 * co, 9 * co))
    out, gvol, g1, g2 = pl.pallas_call(
        functools.partial(kernel, n, planes, height, width, ci, cm, co, scale),
        out_shape=(
            jax.ShapeDtypeStruct((cells, co), F32),
            jax.ShapeDtypeStruct((cells // 2, 2 * ci), F32),
            jax.ShapeDtypeStruct((27, cm // n, ci), F32),
            jax.ShapeDtypeStruct((27, co // n, cm), F32),
        ),
        in_specs=[hbm, hbm, hbm, hbm],
        out_specs=(hbm, hbm, vmem, vmem),
        scratch_shapes=[
            pltpu.VMEM((cells, co), F32),
            pltpu.VMEM((cells // 2, 2 * ci), F32),
            pltpu.VMEM((planes + 2, height // 2 + 1, 2, width, 2 * ci), BF16),
            pltpu.VMEM((planes + 2, height // 2 + 1, 2, width, 2 * cm), BF16),
            pltpu.VMEM((planes + 2, height // 2 + 1, 2, width, 2 * cm), BF16),
            pltpu.VMEM((planes, pad, co), BF16),
            pltpu.VMEM((cells, ci), BF16),
            pltpu.VMEM((2, plane // 2, 2 * cm), BF16),
            pltpu.VMEM((2, plane // 2, 2 * cm), BF16),
            pltpu.VMEM((cells, cm), F32),
            pltpu.VMEM((cells, cm), F32),
            pltpu.VMEM((cells, cm), F32),
            pltpu.VMEM((3 * co, cells), BF16),
            pltpu.VMEM((3 * cm, cells), BF16),
            pltpu.VMEM((3, 3 * cm, 4 * ci), F32),
            pltpu.VMEM((3, 3 * co, 4 * cm), F32),
            pltpu.VMEM((9, 3 * ci, cm), BF16),
            pltpu.VMEM((9, 3 * cm, co), BF16),
            pltpu.VMEM((3, 4 * ci, 3 * cm), BF16),
            pltpu.VMEM((3, 4 * cm, 3 * ci), BF16),
            pltpu.VMEM((3, 4 * cm, 3 * co), BF16),
            pltpu.VMEM((9 * co, 3 * cm), BF16),
            pltpu.VMEM((2, n // 2, rows1, 2 * ci), F32),
            pltpu.VMEM((n // 2, rows1, 2 * ci), F32),
            pltpu.VMEM((n // 2, rows1, 2 * ci), BF16),
            pltpu.VMEM((n // 2, rows1, 2 * ci), BF16),
            pltpu.VMEM((2, n // 2, rows2, 2 * ci), F32),
            pltpu.VMEM((2, n // 2, rows2, 2 * ci), BF16),
            pltpu.VMEM((n // 2, rows2, 2 * ci), BF16),
            pltpu.VMEM((n // 2, rows2, 2 * ci), BF16),
            pltpu.VMEM((n // 2, rows2, 2 * ci), BF16),
            pltpu.SemaphoreType.DMA((3 + planes,)),
            pltpu.SemaphoreType.DMA((planes + 1,)),
            pltpu.SemaphoreType.DMA((4, 2)),
            pltpu.SemaphoreType.DMA((4, 2)),
            pltpu.SemaphoreType.DMA((2,)),
            pltpu.SemaphoreType.DMA((2,)),
            pltpu.SemaphoreType.DMA((2, n // 2)),
            pltpu.SemaphoreType.DMA((2, n // 2)),
        ],
        compiler_params=pltpu.CompilerParams(
            collective_id=0, has_side_effects=True, vmem_limit_bytes=60 << 20
        ),
    )(
        volume.reshape(cells, ci), cotangent.reshape(cells, co), w1, w2
    )
    shapes = [x.shape for x in (out, gvol, g1, g2)]
    shapes[1:2] = [(cells, ci)]
    kept = shapes[:1] + [gvol.shape] + shapes[1:]
    out, gvol, g1, g2 = pl.pallas_call(
        hand_over,
        out_shape=tuple(jax.ShapeDtypeStruct(x, F32) for x in shapes),
        in_specs=[hbm] * 4,
        out_specs=(hbm,) * 4,
        scratch_shapes=[pltpu.VMEM(x, F32) for x in kept]
        + [pltpu.SemaphoreType.DMA((10,)), pltpu.SemaphoreType.DMA((14,))],
        compiler_params=pltpu.CompilerParams(vmem_limit_bytes=60 << 20),
    )(out, gvol, g1, g2)
    return (
        out.reshape(planes, height, width, co),
        gvol.reshape(planes, height, width, ci),
        jnp.transpose(g1.reshape(3, 3, 3, cm // n, ci), (0, 1, 2, 4, 3)),
        jnp.transpose(g2.reshape(3, 3, 3, co // n, cm), (0, 1, 2, 4, 3)),
    )


def solution(mesh):
    return jax.shard_map(
        shards,
        mesh=mesh,
        in_specs=(
            P(("groups", "space"), None, None, None),
            P(),
            P(),
            P(("groups", "space"), None, None, None),
        ),
        out_specs=(
            P(("groups", "space"), None, None, None),
            P(("groups", "space"), None, None, None),
            P("groups", None, None, None, "space"),
            P("groups", None, None, None, "space"),
        ),
        check_vma=False,
    )
```
